32 devices in a mesh: cam: 4 (over y, x), dev: 8 (over z, core).
Axes of the slice: x: 2, y: 2, z: 4, core: 2. Of those that a mesh axis runs over, the one named last changes fastest.
Arguments:
- params: float32 [256, 59, 128], P('dev'), may hold values from -4 to 4
- moment_first: float32 [8, 4, 8, 59, 128], P('dev', 'cam'), may hold values from -3 to 3
- moment_second: float32 [8, 4, 8, 59, 128], P('dev', 'cam'), may hold values from 0.01 to 1
- cam_proj: float32 [8, 9, 59], P('cam'), may hold values from -0.75 to 0.75
- send_block: int32 [8, 8, 8, 2], P('cam', 'dev'), may hold values from 0 to 31
- tile_slot: int32 [8, 16, 8], P('cam', 'dev'), may hold values from 0 to 15, as said below
- tile_count: int32 [8, 16], P('cam', 'dev'), may hold values from 2 to 8, as said below
- targets: float32 [8, 16, 3, 256], P('cam', 'dev'), may hold values from 0 to 1
- split_block: int32 [8, 8], P('dev'), may hold values from 0 to 31, as said below
- split_live: int32 [8, 8], P('dev'), may hold values from 0 to 1, as said below
Outputs:
- images: float32 [8, 16, 3, 256], P('cam', 'dev')
- new_params: float32 [256, 59, 128], P('dev')
- new_first: float32 [8, 4, 8, 59, 128], P('dev', 'cam')
- new_second: float32 [8, 4, 8, 59, 128], P('dev', 'cam')
- children: float32 [64, 2, 59, 128], P('dev')
The draws below stay inside these ranges and needn't reach their ends.
Inputs may be any that keep to these rules, and one draw needn't show every extreme that they name: `tile_count`: in every camera some tile has exactly 8 live entries. `tile_slot`: the entries of one tile's list are distinct; entries at positions from the tile's count on are not read. `split_block`: among an owner's entries where split_live is 1 the blocks are distinct. `split_live`: each row holds exactly 2 ones; in every draw some new owner has a one in every row.
All inputs are finite; a program needn't handle non-finite values.
Results may differ from the reference program's by a relative error of at most 0.0003.
Values sent between devices are 32-bit elements; how exact they have to be, the bound alone decides.
A program may use at most 64 MiB of HBM per device.

```python
import math
import jax
import jax.numpy as jnp
from jax import lax

F = 59
SPL = 128
TSIDE = 16
PIX = 256
PROJ = 9
KMAX = 8
BLK_DEV = 32
TILE_DEV = 2
OWNERS = 8
GROUPS = 4
CAMERAS = 8
TILES = 16
NBLK = 256
BQ = 8
CAP = 2
SLOTS = 16
SPLIT_DEV = 2


def depth_lists(key):
    folded = jax.random.fold_in(key, 7101)
    key_level, key_heavy, key_count, key_order = jax.random.split(folded, 4)
    load_level = jax.random.randint(key_level, (CAMERAS, OWNERS), max(1, KMAX // 2), KMAX + 1)
    heavy_owner = jax.random.randint(key_heavy, (CAMERAS, 1), 0, OWNERS)
    owner_ids = jnp.arange(OWNERS, dtype=jnp.int32)[None, :]
    load_level = jnp.where(owner_ids == heavy_owner, KMAX, load_level)
    lowest = jnp.maximum(load_level // 2, 1)
    tile_counts = jax.random.randint(key_count, (CAMERAS, OWNERS, TILE_DEV), lowest[:, :, None], load_level[:, :, None] + 1)
    first_tile = jnp.arange(TILE_DEV, dtype=jnp.int32)[None, None, :] == 0
    tile_counts = jnp.where((owner_ids[:, :, None] == heavy_owner[:, :, None]) & first_tile, KMAX, tile_counts)
    tile_counts = tile_counts.reshape(CAMERAS, TILES).astype(jnp.int32)
    scores = jax.random.randint(key_order, (CAMERAS, TILES, SLOTS), 0, 1 << 20) * SLOTS + jnp.arange(SLOTS, dtype=jnp.int32)
    slot_order = jnp.argsort(scores, axis=-1)[:, :, :KMAX].astype(jnp.int32)
    return (slot_order, tile_counts)


def draw_tile_slot(key, part):
    return depth_lists(key)[0]


def draw_tile_count(key, part):
    return depth_lists(key)[1]


def split_plan(key):
    folded = jax.random.fold_in(key, 7202)
    key_popular, key_target, key_rank, key_block = jax.random.split(folded, 4)
    popular = jax.random.randint(key_popular, (OWNERS,), 0, 4)
    favoured = jax.random.randint(key_target, (), 0, OWNERS)
    owner_ids = jnp.arange(OWNERS, dtype=jnp.int32)
    popular = jnp.where(owner_ids == favoured, 4, popular)
    scores = (popular[None, :] * (1 << 16) + jax.random.randint(key_rank, (OWNERS, OWNERS), 0, 1 << 16)) * OWNERS + owner_ids[None, :]
    dest_rank = jnp.argsort(jnp.argsort(-scores, axis=1), axis=1).astype(jnp.int32)
    live_mask = (dest_rank < SPLIT_DEV).astype(jnp.int32)
    block_scores = jax.random.randint(key_block, (OWNERS, BLK_DEV), 0, 1 << 20) * BLK_DEV + jnp.arange(BLK_DEV, dtype=jnp.int32)[None, :]
    blocks = jnp.argsort(block_scores, axis=1).astype(jnp.int32)
    chosen = jnp.take_along_axis(blocks, dest_rank % BLK_DEV, axis=1)
    return (chosen.astype(jnp.int32), live_mask)


def draw_split_block(key, part):
    return split_plan(key)[0]


def draw_split_live(key, part):
    return split_plan(key)[1]


def set_ends(array, own_key, low, high):
    shape = array.shape
    index_at = [jax.random.randint(jax.random.fold_in(own_key, axis), (), 0, shape[axis]) for axis in range(len(shape))]
    array = array.at[tuple(index_at)].set(low)
    longest = shape.index(max(shape))
    index_at[longest] = (index_at[longest] + 1) % shape[longest]
    return array.at[tuple(index_at)].set(high)


def steps_of(rng, extent, shards, smallest, high):
    gain, own = 1.0, jax.random.fold_in(rng, 6)
    for position, blocks in shards:
        heights = jnp.exp(jax.random.uniform(jax.random.fold_in(own, position), (blocks,), jnp.float32, smallest / len(shards), high / len(shards)))
        gain = gain * jnp.repeat(heights, extent[position] // blocks).reshape([-1 if axis == position else 1 for axis in range(len(extent))])
    return gain


def centred(rng, dims, deviation, reach, cuts=(), kind=jnp.bfloat16):
    result = deviation * jax.random.normal(rng, dims, jnp.float32)
    if cuts:
        result = result * steps_of(rng, dims, cuts, -0.22, 0.18)
    return jnp.clip(result, -reach, reach).astype(kind)


def setup_inputs(seed: int = 0) -> dict:
    streams_of = jax.random.split(jax.random.key(seed), 11)
    params = centred(streams_of[0], (NBLK, F, SPL), 1.0, 4.0, ((0, 8),), jnp.float32)
    moment_first = centred(streams_of[1], (OWNERS, GROUPS, BQ, F, SPL), 0.5, 3.0, ((0, 8), (1, 4)), jnp.float32)
    moment_second = jnp.clip(jnp.exp(math.log(1.0) - 4.6051702 * jax.random.uniform(streams_of[2], (OWNERS, GROUPS, BQ, F, SPL), jnp.float32) ** steps_of(streams_of[2], (OWNERS, GROUPS, BQ, F, SPL), ((0, 8), (1, 4)), -0.2, 0.2)), 0.01, 1.0)
    cam_proj = centred(streams_of[3], (CAMERAS, PROJ, F), F ** -0.5, 0.75, ((0, 4),), jnp.float32)
    send_block = set_ends(jax.random.randint(streams_of[4], (CAMERAS, OWNERS, OWNERS, CAP), 0, BLK_DEV), jax.random.fold_in(streams_of[4], 1), 0, BLK_DEV - 1).astype(jnp.int32)
    tile_slot = draw_tile_slot(jax.random.fold_in(streams_of[10], 71), 0)
    tile_count = draw_tile_count(jax.random.fold_in(streams_of[10], 71), 0)
    targets = jnp.clip(1.0 * jax.random.uniform(streams_of[7], (CAMERAS, TILES, 3, PIX), jnp.float32) ** steps_of(streams_of[7], (CAMERAS, TILES, 3, PIX), ((0, 4), (1, 8)), -0.2, 0.2), 0.0, 1.0)
    split_block = draw_split_block(jax.random.fold_in(streams_of[10], 71), 0)
    split_live = draw_split_live(jax.random.fold_in(streams_of[10], 71), 0)
    return {"params": params, "moment_first": moment_first, "moment_second": moment_second, "cam_proj": cam_proj, "send_block": send_block, "tile_slot": tile_slot, "tile_count": tile_count, "targets": targets, "split_block": split_block, "split_live": split_live}


LOSS_WEIGHT = 256.0
RATE = 0.01
BETA_FIRST = 0.9
BETA_SECOND = 0.999
EPSILON = 1e-08
SHRINK = math.log(1.6)
PRECISE = lax.Precision.HIGHEST

def unpack(projected):
    centre = 0.5 * TSIDE
    spread = 0.375 * TSIDE
    mean_x = centre + spread * jnp.tanh(projected[:, 0])
    mean_y = centre + spread * jnp.tanh(projected[:, 1])
    conic_a = 0.02 + 0.1 * jax.nn.softplus(projected[:, 2])
    conic_c = 0.02 + 0.1 * jax.nn.softplus(projected[:, 4])
    conic_b = 0.9 * jnp.sqrt(conic_a * conic_c) * jnp.tanh(projected[:, 3])
    opacity = 0.99 * jax.nn.sigmoid(projected[:, 5] - 6.0)
    shape_part = jnp.stack([mean_x, mean_y, conic_a, conic_b, conic_c, opacity], axis=1)
    return jnp.concatenate([shape_part, jax.nn.sigmoid(projected[:, 6:9])], axis=1)

def project(params, matrix):
    projected = jnp.einsum('pf,bfs->bps', matrix, params, precision=PRECISE)
    return unpack(projected)

def footprint(features, active, grid_x, grid_y):
    off_x = grid_x[None, None, :] - features[:, 0, :, None]
    off_y = grid_y[None, None, :] - features[:, 1, :, None]
    exponent = 0.5 * (features[:, 2, :, None] * off_x * off_x + 2.0 * features[:, 3, :, None] * off_x * off_y + features[:, 4, :, None] * off_y * off_y)
    falloff = jnp.exp(-exponent) * active[:, None, None]
    alpha_term = features[:, 5, :, None] * falloff
    return (off_x, off_y, falloff, alpha_term)

def divide(parents):
    offset = 0.5 * jnp.exp(parents[:, 3:6] - 1.0)
    shrunk = parents[:, 3:6] - SHRINK
    remainder = parents[:, 6:]
    child_plus = jnp.concatenate([parents[:, 0:3] + offset, shrunk, remainder], axis=1)
    child_minus = jnp.concatenate([parents[:, 0:3] - offset, shrunk, remainder], axis=1)
    return jnp.stack([child_plus, child_minus], axis=1)

def reference(params, moment_first, moment_second, cam_proj, send_block, tile_slot, tile_count, targets, split_block, split_live):
    pixel_ids = jnp.arange(TSIDE * TSIDE, dtype=jnp.int32)
    grid_x = (pixel_ids % TSIDE).astype(jnp.float32) + 0.5
    grid_y = (pixel_ids // TSIDE).astype(jnp.float32) + 0.5
    owner_ids = jnp.arange(TILES, dtype=jnp.int32) // TILE_DEV
    source_ids = (tile_slot // CAP).astype(jnp.int32)
    within_ids = (tile_slot % CAP).astype(jnp.int32)
    camera_ids = jnp.arange(CAMERAS, dtype=jnp.int32)[:, None, None]
    block_of = (source_ids * BLK_DEV + send_block[camera_ids, source_ids, owner_ids[None, :, None], within_ids]).astype(jnp.int32)
    live_rows = (jnp.arange(KMAX, dtype=jnp.int32)[None, None, :] < tile_count[:, :, None]).astype(jnp.float32)

    def tile_group(features_all, group_blocks, group_live):

        def advance(state_carry, inputs):
            transmit, colour = state_carry
            blocks_now, live_now = inputs
            features = jnp.take(features_all, blocks_now, axis=0)
            unused_x, unused_y, unused_fall, alpha_term = footprint(features, live_now, grid_x, grid_y)
            log_keep = jnp.log1p(-alpha_term)
            log_before = jnp.cumsum(log_keep, axis=1) - log_keep
            weights = alpha_term * transmit[:, None, :] * jnp.exp(log_before)
            colour = colour + jnp.einsum('dcs,dsp->dcp', features[:, 6:9], weights, precision=PRECISE)
            transmit = transmit * jnp.exp(lax.optimization_barrier(jnp.sum(log_keep, axis=1)))
            return ((transmit, colour), None)
        tile_rows = group_blocks.shape[0]
        start_state = (jnp.ones((tile_rows, PIX), jnp.float32), jnp.zeros((tile_rows, 3, PIX), jnp.float32))
        scanned = lax.scan(jax.checkpoint(advance), start_state, (group_blocks.T, group_live.T))
        return scanned[0][1]

    def loss_all(values):

        def per_camera(inputs):
            matrix, blocks_cam, live_cam, target_cam = inputs
            features_all = project(values, matrix)

            def per_group(group_data):
                return tile_group(features_all, group_data[0], group_data[1])
            grouped = lax.map(jax.checkpoint(per_group), (blocks_cam.reshape(OWNERS, TILE_DEV, KMAX), live_cam.reshape(OWNERS, TILE_DEV, KMAX)))
            colour = grouped.reshape(TILES, 3, PIX)
            error = colour - target_cam
            return (0.5 * LOSS_WEIGHT * jnp.sum(error * error), colour)
        losses, colours = lax.map(jax.checkpoint(per_camera), (cam_proj, block_of, live_rows, targets))
        return (jnp.sum(losses), colours)
    gradient, images = jax.grad(loss_all, has_aux=True)(params)
    first_moment = moment_first.reshape(params.shape)
    second_moment = moment_second.reshape(params.shape)
    new_first = BETA_FIRST * first_moment + (1.0 - BETA_FIRST) * gradient
    new_second = BETA_SECOND * second_moment + (1.0 - BETA_SECOND) * gradient * gradient
    new_params = params - RATE * new_first / (jnp.sqrt(new_second) + EPSILON)
    parent_ids = (jnp.arange(OWNERS, dtype=jnp.int32)[None, :] * BLK_DEV + split_block.T).astype(jnp.int32)
    live_mask = split_live.T.reshape(-1).astype(jnp.float32)
    parents = jnp.take(new_params, parent_ids.reshape(-1), axis=0)
    children = divide(parents) * live_mask[:, None, None, None]
    return (images, new_params, new_first.reshape(moment_first.shape), new_second.reshape(moment_second.shape), children)
```

```python
import functools
import math

import jax
import jax.numpy as jnp
from jax import lax
from jax.experimental import pallas as pl
from jax.experimental.pallas import tpu as pltpu
from jax.sharding import PartitionSpec as P

TSIDE = 16
PROJ = 9
PAIR = 2
LOSS_WEIGHT = 256.0
RATE = 0.01
BETA_FIRST = 0.9
BETA_SECOND = 0.999
EPSILON = 1e-08
SHRINK = math.log(1.6)
LOG2E = math.log2(math.e)
MESH = pl.DeviceIdType.MESH
F32 = jnp.float32
BF16 = jnp.bfloat16
VMEM = pl.BlockSpec(memory_space=pltpu.VMEM)
SMEM = pl.BlockSpec(memory_space=pltpu.SMEM)
ANY = pl.BlockSpec(memory_space=pl.ANY)
BIG = 60 * 1024 * 1024
HALF = 128
SAVED = 14


def padded(size, unit):
    return -(-size // unit) * unit


def split2(value):
    high = value.astype(BF16)
    return high, (value - high.astype(F32)).astype(BF16)


def dot32(left, right, dims=(((1,), (0,)), ((), ()))):
    return lax.dot_general(left, right, dims, preferred_element_type=F32)


def softplus(value):
    return jnp.maximum(value, 0.0) + jnp.log(1.0 + jnp.exp(-jnp.abs(value)))


def sigmoid(value):
    return 1.0 / (1.0 + jnp.exp(-value))


def left3(value, width):
    high, low = split2(value)
    high = high.astype(F32)[:, :width]
    low = low.astype(F32)[:, :width]
    return jnp.concatenate([high, low, high], axis=1).astype(BF16)


def right3(value):
    high, low = split2(value)
    return jnp.concatenate([high, high, low], axis=0)


def send(src, dst, send_sem, recv_sem, axis, peer):
    copy = pltpu.make_async_remote_copy(
        src_ref=src,
        dst_ref=dst,
        send_sem=send_sem,
        recv_sem=recv_sem,
        device_id={axis: peer},
        device_id_type=MESH,
    )
    copy.start()
    return copy


def keep(src, dst, sem):
    copy = pltpu.make_async_copy(src, dst, sem)
    copy.start()
    return copy


def make_features(raw_ref, camera, place, cap, feats, saved):
    index = camera * cap + place
    raw = [raw_ref[index, k] for k in range(PROJ)]
    centre = 0.5 * TSIDE
    spread = 0.375 * TSIDE
    turn_x = jnp.tanh(raw[0])
    turn_y = jnp.tanh(raw[1])
    conic_a = 0.02 + 0.1 * softplus(raw[2])
    conic_c = 0.02 + 0.1 * softplus(raw[4])
    turn_b = jnp.tanh(raw[3])
    root = jnp.sqrt(conic_a * conic_c)
    conic_b = 0.9 * root * turn_b
    owners, splats = raw[0].shape
    flat = feats.reshape(feats.shape[0] * 16, splats)

    def put(k, value):
        first = (camera * cap * owners + place) * 16 + k
        flat[pl.ds(first, owners, stride=cap * 16), :] = value

    put(0, centre + spread * turn_x)
    put(1, centre + spread * turn_y)
    put(2, (0.5 * LOG2E) * conic_a)
    put(3, LOG2E * conic_b)
    put(4, (0.5 * LOG2E) * conic_c)
    put(5, math.log2(0.99) - LOG2E * softplus(6.0 - raw[5]))
    saved[index, 0] = conic_a
    saved[index, 1] = conic_b
    saved[index, 2] = conic_c
    saved[index, 3] = spread * (1.0 - turn_x * turn_x)
    saved[index, 4] = spread * (1.0 - turn_y * turn_y)
    saved[index, 5] = 0.1 * sigmoid(raw[2])
    saved[index, 6] = 0.9 * root * (1.0 - turn_b * turn_b)
    saved[index, 7] = 0.1 * sigmoid(raw[4])
    saved[index, 8] = sigmoid(6.0 - raw[5])
    saved[index, 9] = 0.5 * conic_b / conic_a
    saved[index, 10] = 0.5 * conic_b / conic_c
    for k in range(3):
        tone = sigmoid(raw[6 + k])
        put(8 + k, tone)
        saved[index, 11 + k] = tone * (1.0 - tone)


def return_planes(sums, saved, index, back):
    sum0, sum_x, sum_y, sum_xx, sum_xy, sum_yy = sums[:6]
    part = lambda k: saved[index, k]
    grad_b = -sum_xy
    back[index, 0] = (part(0) * sum_x + part(1) * sum_y) * part(3)
    back[index, 1] = (part(1) * sum_x + part(2) * sum_y) * part(4)
    back[index, 2] = (grad_b * part(9) - 0.5 * sum_xx) * part(5)
    back[index, 3] = grad_b * part(6)
    back[index, 4] = (grad_b * part(10) - 0.5 * sum_yy) * part(7)
    back[index, 5] = sum0 * part(8)
    for k in range(3):
        back[index, 6 + k] = sums[6 + k] * part(11 + k)


def render_tile(
    camera, tile, slot_ref, count_ref, target_ref, image_ref,
    feats, entries, weights, pairs, ratios, carry, before, after_tri, cot_rows, cot_cols,
    picture,
):
    depth = slot_ref.shape[2]
    splats = feats.shape[2]
    slots = feats.shape[0] // slot_ref.shape[0]
    pixels = TSIDE * TSIDE
    chunks = pixels // HALF
    per_chunk = HALF // TSIDE
    steps = depth // PAIR
    grid = lax.broadcasted_iota(jnp.int32, (TSIDE, splats), 0).astype(F32) + 0.5
    pad_rows = jnp.zeros((8, splats), F32)
    live = count_ref[camera, tile]
    carry[...] = jnp.zeros(carry.shape, F32)
    picture[...] = jnp.zeros(picture.shape, F32)

    def entry_of(place):
        slot = jnp.clip(slot_ref[camera, tile, place], 0, slots - 1)
        return feats[camera * slots + slot]

    def forward(pair, _):
        places = [PAIR * pair + sub for sub in range(PAIR)]
        alphas, logs, sums, shades = [], [], [], []
        for place in places:
            entry = entry_of(place)
            part = lambda k: entry[k : k + 1]
            off_x = grid - part(0)
            off_y = grid - part(1)
            in_x = -(part(2) * off_x * off_x)
            cross = -(part(3) * off_x)
            faint = part(5) + jnp.where(place < live, 0.0, -1e30)
            in_y = faint - part(4) * off_y * off_y
            for chunk in range(chunks):
                lines = []
                for line in range(chunk * per_chunk, (chunk + 1) * per_chunk):
                    lines.append(in_x + (in_y[line : line + 1] + cross * off_y[line : line + 1]))
                alpha = jnp.exp2(jnp.concatenate(lines, axis=0))
                log_keep = jnp.log2(1.0 - alpha)
                alphas.append(alpha)
                logs.append(log_keep)
                sums.append(dot32(jnp.concatenate(split2(log_keep), axis=1), before[...]))
            colour_high, colour_low = split2(entry[8:16])
            colour_high = colour_high.astype(F32)
            colour_low = colour_low.astype(F32)
            shades.append(
                jnp.concatenate(
                    [
                        jnp.concatenate([colour_high, colour_low], axis=0),
                        jnp.concatenate([colour_high, pad_rows], axis=0),
                    ],
                    axis=1,
                ).astype(BF16)
            )
        for chunk in range(chunks):
            where = slice(chunk * HALF, (chunk + 1) * HALF)
            held = carry[where, :]
            drawn = jnp.zeros((16, HALF), F32)
            for sub, place in enumerate(places):
                at = sub * chunks + chunk
                weight = alphas[at] * jnp.exp2(sums[at][:, :splats] + held)
                held = held + sums[at][:, splats:]
                both = jnp.concatenate(split2(weight), axis=1)
                weights[place, where, :] = weight
                pairs[place, where, :] = both
                ratios[place, where, :] = alphas[at] * jnp.exp2(-logs[at])
                drawn += dot32(shades[sub], both, (((1,), (1,)), ((), ())))
            carry[where, :] = held
            picture[:, where] += drawn[:8] + drawn[8:]
        return 0

    lax.fori_loop(0, steps, forward, 0)
    for k in range(3):
        colour = picture[k : k + 1, :]
        image_ref[camera, k, pl.ds(tile, 1), :] = colour
        picture[k : k + 1, :] = LOSS_WEIGHT * (colour - target_ref[camera, k, pl.ds(tile, 1), :])
    cot_high, cot_low = split2(picture[...])
    cot_high = cot_high.astype(F32)
    cot_low = cot_low.astype(F32)
    cot_rows[...] = jnp.concatenate([cot_high, cot_low], axis=0).astype(BF16)
    stacked = jnp.concatenate(
        [cot_high, cot_low, cot_high, jnp.zeros((HALF - 24, pixels), F32)], axis=0
    )
    cot_cols[...] = stacked.T.astype(BF16)
    carry[...] = jnp.zeros(carry.shape, F32)

    def backward(reverse, _):
        places = [PAIR * (steps - 1 - reverse) + PAIR - 1 - sub for sub in range(PAIR)]
        offsets, shaded, sums = [], [], []
        for place in places:
            entry = entry_of(place)
            part = lambda k: entry[k : k + 1]
            offsets.append((grid - part(0), grid - part(1)))
            colour_high, colour_low = split2(entry[8:16])
            colour_high = colour_high.astype(F32)
            shades = jnp.concatenate(
                [
                    colour_high,
                    colour_high,
                    colour_low.astype(F32),
                    jnp.zeros((HALF - 24, splats), F32),
                ],
                axis=0,
            ).astype(BF16)
            for chunk in range(chunks):
                where = slice(chunk * HALF, (chunk + 1) * HALF)
                piece = dot32(cot_cols[where, :], shades) * weights[place, where, :]
                shaded.append(piece)
                sums.append(dot32(jnp.concatenate(split2(piece), axis=1), after_tri[...]))
        totals = [[jnp.zeros((TSIDE, splats), F32)] * 3 for _ in places]
        for chunk in range(chunks):
            where = slice(chunk * HALF, (chunk + 1) * HALF)
            held = carry[where, :]
            for sub, place in enumerate(places):
                at = sub * chunks + chunk
                pull = shaded[at] - (sums[at][:, :splats] + held) * ratios[place, where, :]
                held = held + sums[at][:, splats:]
                total0, total1, total2 = totals[sub]
                off_y = offsets[sub][1]
                for line in range(per_chunk):
                    height = off_y[chunk * per_chunk + line : chunk * per_chunk + line + 1]
                    piece = pull[line * TSIDE : (line + 1) * TSIDE]
                    lifted = piece * height
                    total0 += piece
                    total1 += lifted
                    total2 += lifted * height
                totals[sub] = [total0, total1, total2]
            carry[where, :] = held
        sum_of = lambda value: jnp.sum(value, axis=0, keepdims=True)
        for sub, place in enumerate(places):
            total0, total1, total2 = totals[sub]
            off_x = offsets[sub][0]
            wide = total0 * off_x
            tinted = dot32(cot_rows[...], pairs[place])
            tinted = tinted[:8, :splats] + tinted[8:, :splats] + tinted[:8, splats:]
            rows = [
                sum_of(total0),
                sum_of(wide),
                sum_of(total1),
                sum_of(wide * off_x),
                sum_of(total1 * off_x),
                sum_of(total2),
            ] + [tinted[k : k + 1] for k in range(3)]
            at = tile * depth + place
            for k in range(PROJ):
                entries[k, pl.ds(at, 1), :] = rows[k]
        return 0

    lax.fori_loop(0, steps, backward, 0)


def adam(gradient, value, first, second):
    new_first = BETA_FIRST * first + (1.0 - BETA_FIRST) * gradient
    new_second = BETA_SECOND * second + (1.0 - BETA_SECOND) * gradient * gradient
    return value - RATE * new_first / (jnp.sqrt(new_second) + EPSILON), new_first, new_second


def step_kernel(
    send_ref, slot_ref, count_ref, split_ref, live_ref, target_ref, proj_ref,
    params_hbm, first_hbm, second_hbm,
    image_ref, params_out, moments_out, child_out,
    meta, blocks, moments, parcels, raw, feats, saved, entries, back, gathered, table,
    fresh, new_moments, parents, landed, children,
    weights, pairs, ratios, carry, before, after_tri, cot_rows, cot_cols, picture,
    load_sems, meta_sems, moment_sems, raw_sems, back_sems, cross_sems, parent_sems, out_sems,
    child_sems, own_sems,
):
    cameras, _, cap, owners = send_ref.shape
    _, tiles, depth = slot_ref.shape
    values, owned, splats = params_hbm.shape
    share = first_hbm.shape[1]
    groups = meta.shape[0]
    me = lax.axis_index("dev")
    group = lax.axis_index("cam")
    slots = cap * owners
    lists = tiles * depth
    pad = padded(values, 16)
    rows = groups * cameras * PROJ
    high_rows = table.shape[1]
    flat_table = table.reshape(owned * high_rows, splats)
    peer_dev = [lax.rem(me + step, owners) for step in range(owners)]
    from_dev = [lax.rem(me - step + owners, owners) for step in range(owners)]
    peer_cam = [lax.rem(group + turn, groups) for turn in range(groups)]
    from_cam = [lax.rem(group - turn + groups, groups) for turn in range(groups)]

    barrier = pltpu.get_barrier_semaphore()
    for step in range(1, owners):
        pl.semaphore_signal(barrier, inc=1, device_id={"dev": peer_dev[step]}, device_id_type=MESH)
    for turn in range(1, groups):
        pl.semaphore_signal(barrier, inc=1, device_id={"cam": peer_cam[turn]}, device_id_type=MESH)

    for block in range(owned):
        blocks[block, values:pad, :] = jnp.zeros((pad - values, splats), F32)
    loads = [
        keep(params_hbm.at[:, block, :], blocks.at[block, pl.ds(0, values), :], load_sems.at[block])
        for block in range(owned)
    ]

    lane = lax.broadcasted_iota(jnp.int32, (8, 128), 1)
    sub = lax.broadcasted_iota(jnp.int32, (8, 128), 0)
    meta[group] = jnp.zeros(meta.shape[1:], F32)
    numbers = jnp.zeros((8, 128), F32)
    for camera in range(cameras):
        for place in range(cap):
            for owner in range(owners):
                number = send_ref[camera, 0, place, owner].astype(F32)
                numbers = jnp.where(
                    (lane == place * owners + owner) & (sub == camera), number, numbers
                )
        for k in range(PROJ):
            meta[group, camera * PROJ + k : camera * PROJ + k + 1, 0:values] = proj_ref[
                k, camera : camera + 1, :
            ]
    meta_rows = meta.shape[1]
    meta[group, meta_rows - 8 : meta_rows, :] = numbers

    matrices = []
    for camera in range(cameras):
        own = meta[group, camera * PROJ : (camera + 1) * PROJ, :]
        own = jnp.concatenate([own, jnp.zeros((16 - PROJ, 128), F32)], axis=0)
        matrices.append(left3(own, pad))

    row = lax.broadcasted_iota(jnp.int32, (splats, splats), 0)
    column = lax.broadcasted_iota(jnp.int32, (splats, splats), 1)
    ones = jnp.ones((splats, splats), BF16)
    lower = jnp.where(row < column, 1.0, 0.0).astype(BF16)
    upper = jnp.where(row > column, 1.0, 0.0).astype(BF16)
    for part in range(2):
        before[part * splats : (part + 1) * splats, :splats] = lower
        before[part * splats : (part + 1) * splats, splats:] = ones
        after_tri[part * splats : (part + 1) * splats, :splats] = upper
        after_tri[part * splats : (part + 1) * splats, splats:] = ones
    feats[...] = jnp.zeros(feats.shape, F32)

    for load in loads:
        load.wait()
    for camera in range(cameras):
        items = [(place, owner) for owner in range(owners) for place in range(cap)]
        for start in range(0, len(items), 2):
            couple = items[start : start + 2]
            right = jnp.concatenate(
                [right3(blocks[send_ref[camera, 0, place, owner]]) for place, owner in couple],
                axis=1,
            )
            result = dot32(matrices[camera], right)
            for number, (place, owner) in enumerate(couple):
                parcels[owner, camera * cap + place] = result[
                    :, number * splats : (number + 1) * splats
                ]

    pl.semaphore_wait(barrier, owners + groups - 2)
    raw_copies = []
    for step in range(1, owners):
        raw_copies.append(
            send(
                parcels.at[peer_dev[step], :, pl.ds(0, PROJ), :], raw.at[:, :, me, :],
                raw_sems.at[0, step - 1], raw_sems.at[1, step - 1], "dev", peer_dev[step],
            )
        )
    own_raw = keep(parcels.at[me, :, pl.ds(0, PROJ), :], raw.at[:, :, me, :], own_sems.at[0])
    meta_copies, moment_copies = [], []
    for turn in range(1, groups):
        meta_copies.append(
            send(
                meta.at[group], meta.at[group],
                meta_sems.at[0, turn - 1], meta_sems.at[1, turn - 1], "cam", peer_cam[turn],
            )
        )
    for turn in range(1, groups):
        for kind, source in enumerate((first_hbm, second_hbm)):
            for place in range(share):
                moment_copies.append(
                    send(
                        source.at[:, place, :],
                        moments.at[kind, group * share + place, pl.ds(0, values), :],
                        moment_sems.at[0, turn - 1, kind, place],
                        moment_sems.at[1, turn - 1, kind, place],
                        "cam", peer_cam[turn],
                    )
                )
    own_moments = [
        keep(
            source.at[:, place, :],
            moments.at[kind, group * share + place, pl.ds(0, values), :],
            moment_sems.at[0, groups - 1, kind, place],
        )
        for kind, source in enumerate((first_hbm, second_hbm))
        for place in range(share)
    ]

    one_hots = []
    entry_lane = lax.broadcasted_iota(jnp.int32, (slots, lists), 1)
    slot_row = lax.broadcasted_iota(jnp.int32, (slots, lists), 0)
    slot_row = lax.rem(slot_row, owners) * cap + lax.div(slot_row, owners)
    for camera in range(cameras):
        ids = jnp.full((slots, lists), -1, jnp.int32)
        for tile in range(tiles):
            for place in range(depth):
                slot = slot_ref[camera, tile, place]
                slot = jnp.where(place < count_ref[camera, tile], slot, -1)
                ids = jnp.where(entry_lane == tile * depth + place, slot, ids)
        hot = jnp.where(ids == slot_row, 1.0, 0.0)
        one_hots.append(jnp.concatenate([hot, hot], axis=1).astype(BF16))

    own_raw.wait()
    for copy in raw_copies:
        copy.wait_recv()
    for camera in range(cameras):
        for place in range(cap):
            make_features(raw, camera, place, cap, feats, saved)

    def render(camera, tile):
        render_tile(
            camera, tile, slot_ref, count_ref, target_ref, image_ref, feats, entries,
            weights, pairs, ratios, carry, before, after_tri, cot_rows, cot_cols, picture,
        )

    def slot_sums(camera):
        planes = []
        for start in range(0, PROJ, 2):
            kinds = list(range(start, min(start + 2, PROJ)))
            right = jnp.concatenate(
                [jnp.concatenate(split2(entries[k]), axis=0) for k in kinds], axis=1
            )
            result = dot32(one_hots[camera], right)
            for number in range(len(kinds)):
                planes.append(result[:, number * splats : (number + 1) * splats])
        for place in range(cap):
            part = [plane[place * owners : (place + 1) * owners] for plane in planes]
            return_planes(part, saved, camera * cap + place, back)

    back_copies = [[] for _ in range(cameras)]
    cross_copies = [[] for _ in range(cameras)]
    own_back = []

    def send_back(camera):
        mine = pl.ds(camera * cap, cap)
        for step in range(1, owners):
            back_copies[camera].append(
                send(
                    back.at[mine, :, peer_dev[step], :], gathered.at[group, mine, :, me, :],
                    back_sems.at[0, camera, step - 1], back_sems.at[1, camera, step - 1],
                    "dev", peer_dev[step],
                )
            )
        own_back.append(
            keep(
                back.at[mine, :, me, :], gathered.at[group, mine, :, me, :], own_sems.at[1 + camera]
            )
        )

    def send_across(camera):
        mine = pl.ds(camera * cap, cap)
        for step in range(owners):
            source = from_dev[step]
            if step:
                back_copies[camera][step - 1].wait_recv()
            else:
                own_back[camera].wait()
            piece = gathered.at[group, mine, :, source, :]
            for turn in range(1, groups):
                cross_copies[camera].append(
                    send(
                        piece, piece,
                        cross_sems.at[0, camera, turn - 1, step],
                        cross_sems.at[1, camera, turn - 1, step],
                        "cam", peer_cam[turn],
                    )
                )

    def scatter(turn, camera):
        origin = from_cam[turn]
        base = meta.shape[1] - 8
        ids = meta[origin, base + camera : base + camera + 1, :][:, :slots]
        block_row = lax.broadcasted_iota(jnp.int32, (owned, slots), 0).astype(F32)
        hot = jnp.where(jnp.broadcast_to(ids, (owned, slots)) == block_row, 1.0, 0.0)
        left = jnp.concatenate([hot, hot], axis=1).astype(BF16)
        for start in range(0, PROJ, 2):
            kinds = list(range(start, min(start + 2, PROJ)))
            sides = []
            for k in kinds:
                plane = jnp.concatenate(
                    [gathered[origin, camera * cap + place, k] for place in range(cap)], axis=0
                )
                sides.append(jnp.concatenate(split2(plane), axis=0))
            result = dot32(left, jnp.concatenate(sides, axis=1))
            for number, k in enumerate(kinds):
                flat_table[pl.ds((turn * cameras + camera) * PROJ + k, owned, stride=high_rows), :] = (
                    result[:, number * splats : (number + 1) * splats]
                )

    for camera in range(cameras):
        for tile in range(tiles):
            render(camera, tile)
            if camera and tile == 0:
                send_across(camera - 1)
        slot_sums(camera)
        send_back(camera)
    table[:, rows:high_rows, :] = jnp.zeros((owned, high_rows - rows, splats), F32)
    for copy in meta_copies:
        copy.wait_recv()
    stack = []
    for turn in range(groups):
        stack.append(meta[from_cam[turn], 0 : cameras * PROJ, :])
    stack.append(jnp.zeros((128 * -(-rows // 128) - rows, 128), F32))
    turned = jnp.concatenate(stack, axis=0).T
    left = left3(turned[:pad], high_rows)
    send_across(cameras - 1)
    for camera in range(cameras):
        scatter(0, camera)
    for camera in range(cameras):
        for turn in range(1, groups):
            for step in range(owners):
                cross_copies[camera][step * (groups - 1) + turn - 1].wait_recv()
            scatter(turn, camera)
    for copy in moment_copies:
        copy.wait_recv()
    for copy in own_moments:
        copy.wait()

    def gradients(couple):
        right = jnp.concatenate([right3(table[block]) for block in couple], axis=1)
        result = dot32(left, right)
        return [result[:, at * splats : (at + 1) * splats] for at in range(len(couple))]

    line = lax.broadcasted_iota(jnp.int32, (pad, splats), 0)
    for start in range(0, owners, 2):
        couple = list(range(start, min(start + 2, owners)))
        chosen = [split_ref[0, owner] for owner in couple]
        for owner, block, gradient in zip(couple, chosen, gradients(chosen)):
            alive = live_ref[0, owner].astype(F32)
            new_value, _, _ = adam(gradient, blocks[block], moments[0, block], moments[1, block])
            new_value = jnp.where(line < values, new_value, 1.0)
            parents[owner] = new_value * alive
    parent_copies = []
    for step in range(1, owners):
        parent_copies.append(
            send(
                parents.at[peer_dev[step], pl.ds(0, values + 1), :],
                landed.at[me, pl.ds(0, values + 1), :],
                parent_sems.at[0, step - 1], parent_sems.at[1, step - 1], "dev", peer_dev[step],
            )
        )
    own_parent = keep(
        parents.at[me, pl.ds(0, values + 1), :], landed.at[me, pl.ds(0, values + 1), :],
        own_sems.at[1 + cameras],
    )
    outs = []
    for start in range(0, owned, 2):
        couple = list(range(start, min(start + 2, owned)))
        for block, gradient in zip(couple, gradients(couple)):
            new_value, new_first, new_second = adam(
                gradient, blocks[block], moments[0, block], moments[1, block]
            )
            fresh[block] = new_value
            new_moments[0, block] = new_first
            new_moments[1, block] = new_second
            outs.append(
                keep(fresh.at[block], params_out.at[block], out_sems.at[block])
            )
    outs.append(
        keep(
            new_moments.at[:, pl.ds(group * share, share)], moments_out, own_sems.at[2 + cameras]
        )
    )
    for step in range(owners):
        source = from_dev[step]
        if step:
            parent_copies[step - 1].wait_recv()
        else:
            own_parent.wait()
        parent = landed[source]
        alive = parent[values : values + 1]
        shift = jnp.concatenate(
            [0.5 * jnp.exp(parent[0:8] - 1.0) * alive], axis=0
        )
        shift = jnp.concatenate([shift[3:6], jnp.zeros((pad - 3, splats), F32)], axis=0)
        shrunk = parent - jnp.where((line >= 3) & (line < 6), SHRINK, 0.0) * alive
        children[source, 0] = shrunk + shift
        children[source, 1] = shrunk - shift
        outs.append(keep(children.at[source], child_out.at[source], child_sems.at[step]))
    for copy in outs:
        copy.wait()
    for copy in raw_copies + meta_copies + moment_copies + parent_copies:
        copy.wait_send()
    for camera in range(cameras):
        for copy in back_copies[camera] + cross_copies[camera]:
            copy.wait_send()


def spread_kernel(
    image_ref, fresh_ref, moments_ref, children_ref,
    image_out, params_out, first_out, second_out, child_out,
    fresh, moments, children, in_sems, out_sems,
):
    owned = fresh.shape[0]
    owners = children.shape[0]
    share = moments.shape[1]
    values = params_out.shape[0]
    lump = 8
    loads, jobs = [], []
    for start in range(0, owned, lump):
        some = pl.ds(start, min(lump, owned - start))
        loads.append((fresh_ref.at[some], fresh.at[some]))
        jobs.append(
            [
                (fresh.at[block, pl.ds(0, values), :], params_out.at[:, block, :])
                for block in range(start, min(start + lump, owned))
            ]
        )
    for start in range(0, owners, lump):
        some = pl.ds(start, min(lump, owners - start))
        loads.append((children_ref.at[some], children.at[some]))
        jobs.append(
            [
                (children.at[source, kind, pl.ds(0, values), :], child_out.at[source, :, kind, :])
                for source in range(start, min(start + lump, owners))
                for kind in range(2)
            ]
        )
    for kind, target in enumerate((first_out, second_out)):
        loads.append((moments_ref.at[kind], moments.at[kind]))
        jobs.append(
            [
                (moments.at[kind, place, pl.ds(0, values), :], target.at[:, place, :])
                for place in range(share)
            ]
        )
    started = [keep(src, dst, in_sems.at[number]) for number, (src, dst) in enumerate(loads)]
    image_out[...] = image_ref[...]
    outs = []
    for copy, job in zip(started, jobs):
        copy.wait()
        for src, dst in job:
            outs.append(keep(src, dst, out_sems.at[len(outs)]))
    for copy in outs:
        copy.wait()


def spread_out(images, fresh, new_moments, children, values):
    owned, pad, splats = fresh.shape
    share = new_moments.shape[1]
    owners = children.shape[0]
    shape = jax.ShapeDtypeStruct
    return pl.pallas_call(
        spread_kernel,
        out_shape=(
            shape(images.shape, F32),
            shape((values, owned, splats), F32),
            shape((values, share, splats), F32),
            shape((values, share, splats), F32),
            shape((owners, values, 2, splats), F32),
        ),
        in_specs=[VMEM, ANY, ANY, ANY],
        out_specs=(VMEM, ANY, ANY, ANY, ANY),
        scratch_shapes=[
            pltpu.VMEM(fresh.shape, F32),
            pltpu.VMEM(new_moments.shape, F32),
            pltpu.VMEM(children.shape, F32),
            pltpu.SemaphoreType.DMA((owned + owners + 2,)),
            pltpu.SemaphoreType.DMA((owned + 2 * owners + 2 * share,)),
        ],
        compiler_params=pltpu.CompilerParams(vmem_limit_bytes=BIG),
        name="spread",
    )(images, fresh, new_moments, children)


def body(
    params, moment_first, moment_second, cam_proj, send_block,
    tile_slot, tile_count, targets, split_block, split_live,
):
    groups = lax.axis_size("cam")
    cameras, _, values = cam_proj.shape
    owned, _, splats = params.shape
    share = moment_first.shape[2]
    owners, cap = send_block.shape[2:]
    _, tiles, depth = tile_slot.shape
    pixels = targets.shape[-1]
    depth = padded(depth, PAIR)
    pad = padded(values, 16)
    indices = cameras * cap
    rows = groups * cameras * PROJ
    high_rows = padded(rows, 16)
    meta_rows = padded(cameras * PROJ, 8) + 8
    by_value = lambda moment: moment[0, 0].transpose(1, 0, 2)
    shape = jax.ShapeDtypeStruct
    dma = pltpu.SemaphoreType.DMA
    scratch = [
        pltpu.VMEM((groups, meta_rows, 128), F32),
        pltpu.VMEM((owned, pad, splats), F32),
        pltpu.VMEM((2, owned, pad, splats), F32),
        pltpu.VMEM((owners, indices, 16, splats), F32),
        pltpu.VMEM((indices, PROJ, owners, splats), F32),
        pltpu.VMEM((indices * owners, 16, splats), F32),
        pltpu.VMEM((indices, SAVED, owners, splats), F32),
        pltpu.VMEM((PROJ, tiles * depth, splats), F32),
        pltpu.VMEM((indices, PROJ, owners, splats), F32),
        pltpu.VMEM((groups, indices, PROJ, owners, splats), F32),
        pltpu.VMEM((owned, high_rows, splats), F32),
        pltpu.VMEM((owned, pad, splats), F32),
        pltpu.VMEM((2, owned, pad, splats), F32),
        pltpu.VMEM((owners, pad, splats), F32),
        pltpu.VMEM((owners, pad, splats), F32),
        pltpu.VMEM((owners, 2, pad, splats), F32),
        pltpu.VMEM((depth, pixels, splats), F32),
        pltpu.VMEM((depth, pixels, 2 * splats), BF16),
        pltpu.VMEM((depth, pixels, splats), F32),
        pltpu.VMEM((pixels, splats), F32),
        pltpu.VMEM((2 * splats, 2 * splats), BF16),
        pltpu.VMEM((2 * splats, 2 * splats), BF16),
        pltpu.VMEM((16, pixels), BF16),
        pltpu.VMEM((pixels, 128), BF16),
        pltpu.VMEM((8, pixels), F32),
        dma((owned,)),
        dma((2, groups - 1)),
        dma((2, groups, 2, share)),
        dma((2, owners - 1)),
        dma((2, cameras, owners - 1)),
        dma((2, cameras, groups - 1, owners)),
        dma((2, owners - 1)),
        dma((owned,)),
        dma((owners,)),
        dma((3 + cameras,)),
    ]
    images, fresh, new_moments, children = pl.pallas_call(
        step_kernel,
        out_shape=(
            shape((cameras, 3, tiles, pixels), F32),
            shape((owned, pad, splats), F32),
            shape((2, share, pad, splats), F32),
            shape((owners, 2, pad, splats), F32),
        ),
        in_specs=[SMEM] * 5 + [VMEM] * 2 + [ANY] * 3,
        out_specs=(VMEM, ANY, ANY, ANY),
        scratch_shapes=scratch,
        compiler_params=pltpu.CompilerParams(
            collective_id=5, has_side_effects=True, vmem_limit_bytes=BIG
        ),
        name="step",
    )(
        send_block.transpose(0, 1, 3, 2), tile_slot, tile_count, split_block, split_live,
        targets.transpose(0, 2, 1, 3), cam_proj.transpose(1, 0, 2),
        params.transpose(1, 0, 2), by_value(moment_first), by_value(moment_second),
    )
    images, new_params, new_first, new_second, children = spread_out(
        images, fresh, new_moments, children, values
    )
    restore = lambda moment: moment.transpose(1, 0, 2).reshape(moment_first.shape)
    return (
        images.transpose(0, 2, 1, 3),
        new_params.transpose(1, 0, 2),
        restore(new_first),
        restore(new_second),
        children.transpose(0, 2, 1, 3),
    )


def solution(mesh):
    placed = (
        P("dev", None, None),
        P("dev", "cam", None, None, None),
        P("dev", "cam", None, None, None),
        P("cam", None, None),
        P("cam", "dev", None, None),
        P("cam", "dev", None),
        P("cam", "dev"),
        P("cam", "dev", None, None),
        P("dev", None),
        P("dev", None),
    )
    return jax.shard_map(
        body,
        mesh=mesh,
        in_specs=placed,
        out_specs=(
            P("cam", "dev", None, None),
            P("dev", None, None),
            P("dev", "cam", None, None, None),
            P("dev", "cam", None, None, None),
            P("dev", None, None, None),
        ),
        check_vma=False,
    )
```

```python
import functools
import math

import jax
import jax.numpy as jnp
from jax import lax
from jax.experimental import pallas as pl
from jax.experimental.pallas import tpu as pltpu
from jax.sharding import PartitionSpec as P

TSIDE = 16
PROJ = 9
PAIR = 4
LOSS_WEIGHT = 256.0
RATE = 0.01
BETA_FIRST = 0.9
BETA_SECOND = 0.999
EPSILON = 1e-08
SHRINK = math.log(1.6)
LOG2E = math.log2(math.e)
MESH = pl.DeviceIdType.MESH
F32 = jnp.float32
BF16 = jnp.bfloat16
VMEM = pl.BlockSpec(memory_space=pltpu.VMEM)
SMEM = pl.BlockSpec(memory_space=pltpu.SMEM)
ANY = pl.BlockSpec(memory_space=pl.ANY)
BIG = 60 * 1024 * 1024
HALF = 128
SAVED = 14


def padded(size, unit):
    return -(-size // unit) * unit


def split2(value):
    high = value.astype(BF16)
    return high, (value - high.astype(F32)).astype(BF16)


def dot32(left, right, dims=(((1,), (0,)), ((), ()))):
    return lax.dot_general(left, right, dims, preferred_element_type=F32)


def softplus(value):
    return jnp.maximum(value, 0.0) + jnp.log(1.0 + jnp.exp(-jnp.abs(value)))


def sigmoid(value):
    return 1.0 / (1.0 + jnp.exp(-value))


def left3(value, width):
    high, low = split2(value)
    high = high.astype(F32)[:, :width]
    low = low.astype(F32)[:, :width]
    return jnp.concatenate([high, low, high], axis=1).astype(BF16)


def right3(value):
    high, low = split2(value)
    return jnp.concatenate([high, high, low], axis=0)


def send(src, dst, send_sem, recv_sem, axis, peer):
    copy = pltpu.make_async_remote_copy(
        src_ref=src,
        dst_ref=dst,
        send_sem=send_sem,
        recv_sem=recv_sem,
        device_id={axis: peer},
        device_id_type=MESH,
    )
    copy.start()
    return copy


def keep(src, dst, sem):
    copy = pltpu.make_async_copy(src, dst, sem)
    copy.start()
    return copy


def make_features(raw_ref, camera, place, cap, feats, saved):
    index = camera * cap + place
    raw = [raw_ref[index, k] for k in range(PROJ)]
    centre = 0.5 * TSIDE
    spread = 0.375 * TSIDE
    turn_x = jnp.tanh(raw[0])
    turn_y = jnp.tanh(raw[1])
    conic_a = 0.02 + 0.1 * softplus(raw[2])
    conic_c = 0.02 + 0.1 * softplus(raw[4])
    turn_b = jnp.tanh(raw[3])
    root = jnp.sqrt(conic_a * conic_c)
    conic_b = 0.9 * root * turn_b
    owners, splats = raw[0].shape
    flat = feats.reshape(feats.shape[0] * 16, splats)

    def put(k, value):
        first = (camera * cap * owners + place) * 16 + k
        flat[pl.ds(first, owners, stride=cap * 16), :] = value

    put(0, centre + spread * turn_x)
    put(1, centre + spread * turn_y)
    put(2, (0.5 * LOG2E) * conic_a)
    put(3, LOG2E * conic_b)
    put(4, (0.5 * LOG2E) * conic_c)
    put(5, math.log2(0.99) - LOG2E * softplus(6.0 - raw[5]))
    saved[index, 0] = conic_a
    saved[index, 1] = conic_b
    saved[index, 2] = conic_c
    saved[index, 3] = spread * (1.0 - turn_x * turn_x)
    saved[index, 4] = spread * (1.0 - turn_y * turn_y)
    saved[index, 5] = 0.1 * sigmoid(raw[2])
    saved[index, 6] = 0.9 * root * (1.0 - turn_b * turn_b)
    saved[index, 7] = 0.1 * sigmoid(raw[4])
    saved[index, 8] = sigmoid(6.0 - raw[5])
    saved[index, 9] = 0.5 * conic_b / conic_a
    saved[index, 10] = 0.5 * conic_b / conic_c
    for k in range(3):
        tone = sigmoid(raw[6 + k])
        put(8 + k, tone)
        saved[index, 11 + k] = tone * (1.0 - tone)


def return_planes(sums, saved, index, back):
    sum0, sum_x, sum_y, sum_xx, sum_xy, sum_yy = sums[:6]
    part = lambda k: saved[index, k]
    grad_b = -sum_xy
    back[index, 0] = (part(0) * sum_x + part(1) * sum_y) * part(3)
    back[index, 1] = (part(1) * sum_x + part(2) * sum_y) * part(4)
    back[index, 2] = (grad_b * part(9) - 0.5 * sum_xx) * part(5)
    back[index, 3] = grad_b * part(6)
    back[index, 4] = (grad_b * part(10) - 0.5 * sum_yy) * part(7)
    back[index, 5] = sum0 * part(8)
    for k in range(3):
        back[index, 6 + k] = sums[6 + k] * part(11 + k)


def render_tile(
    camera, tile, slot_ref, count_ref, target_ref, image_ref,
    feats, entries, weights, pairs, ratios, carry, before, after_tri, cot_rows, cot_cols,
    picture,
):
    depth = slot_ref.shape[2]
    splats = feats.shape[2]
    slots = feats.shape[0] // slot_ref.shape[0]
    pixels = TSIDE * TSIDE
    chunks = pixels // HALF
    per_chunk = HALF // TSIDE
    steps = depth // PAIR
    grid = lax.broadcasted_iota(jnp.int32, (TSIDE, splats), 0).astype(F32) + 0.5
    pad_rows = jnp.zeros((8, splats), F32)
    live = count_ref[camera, tile]
    carry[...] = jnp.zeros(carry.shape, F32)
    picture[...] = jnp.zeros(picture.shape, F32)

    def entry_of(place):
        slot = jnp.clip(slot_ref[camera, tile, place], 0, slots - 1)
        return feats[camera * slots + slot]

    def forward(pair, _):
        places = [PAIR * pair + sub for sub in range(PAIR)]
        alphas, logs, sums, shades = [], [], [], []
        for place in places:
            entry = entry_of(place)
            part = lambda k: entry[k : k + 1]
            off_x = grid - part(0)
            off_y = grid - part(1)
            in_x = -(part(2) * off_x * off_x)
            cross = -(part(3) * off_x)
            faint = part(5) + jnp.where(place < live, 0.0, -1e30)
            in_y = faint - part(4) * off_y * off_y
            for chunk in range(chunks):
                lines = []
                for line in range(chunk * per_chunk, (chunk + 1) * per_chunk):
                    lines.append(in_x + (in_y[line : line + 1] + cross * off_y[line : line + 1]))
                alpha = jnp.exp2(jnp.concatenate(lines, axis=0))
                log_keep = jnp.log2(1.0 - alpha)
                alphas.append(alpha)
                logs.append(log_keep)
                sums.append(dot32(jnp.concatenate(split2(log_keep), axis=1), before[...]))
            colour_high, colour_low = split2(entry[8:16])
            colour_high = colour_high.astype(F32)
            colour_low = colour_low.astype(F32)
            shades.append(
                jnp.concatenate(
                    [
                        jnp.concatenate([colour_high, colour_low], axis=0),
                        jnp.concatenate([colour_high, pad_rows], axis=0),
                    ],
                    axis=1,
                ).astype(BF16)
            )
        for chunk in range(chunks):
            where = slice(chunk * HALF, (chunk + 1) * HALF)
            held = carry[where, :]
            drawn = jnp.zeros((16, HALF), F32)
            for sub, place in enumerate(places):
                at = sub * chunks + chunk
                weight = alphas[at] * jnp.exp2(sums[at][:, :splats] + held)
                held = held + sums[at][:, splats:]
                both = jnp.concatenate(split2(weight), axis=1)
                weights[place, where, :] = weight
                pairs[place, where, :] = both
                ratios[place, where, :] = alphas[at] * jnp.exp2(-logs[at])
                drawn += dot32(shades[sub], both, (((1,), (1,)), ((), ())))
            carry[where, :] = held
            picture[:, where] += drawn[:8] + drawn[8:]
        return 0

    lax.fori_loop(0, steps, forward, 0)
    for k in range(3):
        colour = picture[k : k + 1, :]
        image_ref[camera, k, pl.ds(tile, 1), :] = colour
        picture[k : k + 1, :] = LOSS_WEIGHT * (colour - target_ref[camera, k, pl.ds(tile, 1), :])
    cot_high, cot_low = split2(picture[...])
    cot_high = cot_high.astype(F32)
    cot_low = cot_low.astype(F32)
    cot_rows[...] = jnp.concatenate([cot_high, cot_low], axis=0).astype(BF16)
    stacked = jnp.concatenate(
        [cot_high, cot_low, cot_high, jnp.zeros((HALF - 24, pixels), F32)], axis=0
    )
    cot_cols[...] = stacked.T.astype(BF16)
    carry[...] = jnp.zeros(carry.shape, F32)

    def backward(reverse, _):
        places = [PAIR * (steps - 1 - reverse) + PAIR - 1 - sub for sub in range(PAIR)]
        offsets, shaded, sums = [], [], []
        for place in places:
            entry = entry_of(place)
            part = lambda k: entry[k : k + 1]
            offsets.append((grid - part(0), grid - part(1)))
            colour_high, colour_low = split2(entry[8:16])
            colour_high = colour_high.astype(F32)
            shades = jnp.concatenate(
                [
                    colour_high,
                    colour_high,
                    colour_low.astype(F32),
                    jnp.zeros((HALF - 24, splats), F32),
                ],
                axis=0,
            ).astype(BF16)
            for chunk in range(chunks):
                where = slice(chunk * HALF, (chunk + 1) * HALF)
                piece = dot32(cot_cols[where, :], shades) * weights[place, where, :]
                shaded.append(piece)
                sums.append(dot32(jnp.concatenate(split2(piece), axis=1), after_tri[...]))
        totals = [[jnp.zeros((TSIDE, splats), F32)] * 3 for _ in places]
        for chunk in range(chunks):
            where = slice(chunk * HALF, (chunk + 1) * HALF)
            held = carry[where, :]
            for sub, place in enumerate(places):
                at = sub * chunks + chunk
                pull = shaded[at] - (sums[at][:, :splats] + held) * ratios[place, where, :]
                held = held + sums[at][:, splats:]
                total0, total1, total2 = totals[sub]
                off_y = offsets[sub][1]
                for line in range(per_chunk):
                    height = off_y[chunk * per_chunk + line : chunk * per_chunk + line + 1]
                    piece = pull[line * TSIDE : (line + 1) * TSIDE]
                    lifted = piece * height
                    total0 += piece
                    total1 += lifted
                    total2 += lifted * height
                totals[sub] = [total0, total1, total2]
            carry[where, :] = held
        sum_of = lambda value: jnp.sum(value, axis=0, keepdims=True)
        for sub, place in enumerate(places):
            total0, total1, total2 = totals[sub]
            off_x = offsets[sub][0]
            wide = total0 * off_x
            tinted = dot32(cot_rows[...], pairs[place])
            tinted = tinted[:8, :splats] + tinted[8:, :splats] + tinted[:8, splats:]
            rows = [
                sum_of(total0),
                sum_of(wide),
                sum_of(total1),
                sum_of(wide * off_x),
                sum_of(total1 * off_x),
                sum_of(total2),
            ] + [tinted[k : k + 1] for k in range(3)]
            at = tile * depth + place
            for k in range(PROJ):
                entries[k, pl.ds(at, 1), :] = rows[k]
        return 0

    lax.fori_loop(0, steps, backward, 0)


def adam(gradient, value, first, second):
    new_first = BETA_FIRST * first + (1.0 - BETA_FIRST) * gradient
    new_second = BETA_SECOND * second + (1.0 - BETA_SECOND) * gradient * gradient
    return value - RATE * new_first / (jnp.sqrt(new_second) + EPSILON), new_first, new_second


def step_kernel(
    send_ref, slot_ref, count_ref, split_ref, live_ref, target_ref, proj_ref,
    params_hbm, first_hbm, second_hbm,
    image_ref, params_out, moments_out, child_out,
    meta, blocks, moments, arrived, parcels, raw, feats, saved, entries, back, gathered, table,
    fresh, new_moments, parents, landed, children,
    weights, pairs, ratios, carry, before, after_tri, cot_rows, cot_cols, picture,
    load_sems, meta_sems, moment_sems, raw_sems, back_sems, cross_sems, parent_sems, out_sems,
    child_sems, own_sems,
):
    cameras, _, cap, owners = send_ref.shape
    _, tiles, depth = slot_ref.shape
    values, owned, splats = params_hbm.shape
    share = first_hbm.shape[1]
    groups = meta.shape[0]
    me = lax.axis_index("dev")
    group = lax.axis_index("cam")
    slots = cap * owners
    lists = tiles * depth
    pad = padded(values, 16)
    rows = groups * cameras * PROJ
    high_rows = table.shape[1]
    flat_table = table.reshape(owned * high_rows, splats)
    peer_dev = [lax.rem(me + step, owners) for step in range(owners)]
    from_dev = [lax.rem(me - step + owners, owners) for step in range(owners)]
    peer_cam = [lax.rem(group + turn, groups) for turn in range(groups)]
    from_cam = [lax.rem(group - turn + groups, groups) for turn in range(groups)]

    barrier = pltpu.get_barrier_semaphore()
    for step in range(1, owners):
        pl.semaphore_signal(barrier, inc=1, device_id={"dev": peer_dev[step]}, device_id_type=MESH)
    for turn in range(1, groups):
        pl.semaphore_signal(barrier, inc=1, device_id={"cam": peer_cam[turn]}, device_id_type=MESH)

    for block in range(owned):
        blocks[block, values:pad, :] = jnp.zeros((pad - values, splats), F32)
    loads = [
        keep(params_hbm.at[:, block, :], blocks.at[block, pl.ds(0, values), :], load_sems.at[block])
        for block in range(owned)
    ]

    lane = lax.broadcasted_iota(jnp.int32, (8, 128), 1)
    sub = lax.broadcasted_iota(jnp.int32, (8, 128), 0)
    meta[group] = jnp.zeros(meta.shape[1:], F32)
    numbers = jnp.zeros((8, 128), F32)
    for camera in range(cameras):
        for place in range(cap):
            for owner in range(owners):
                number = send_ref[camera, 0, place, owner].astype(F32)
                numbers = jnp.where(
                    (lane == place * owners + owner) & (sub == camera), number, numbers
                )
        for k in range(PROJ):
            meta[group, camera * PROJ + k : camera * PROJ + k + 1, 0:values] = proj_ref[
                k, camera : camera + 1, :
            ]
    meta_rows = meta.shape[1]
    meta[group, meta_rows - 8 : meta_rows, :] = numbers

    matrices = []
    for camera in range(cameras):
        own = meta[group, camera * PROJ : (camera + 1) * PROJ, :]
        own = jnp.concatenate([own, jnp.zeros((16 - PROJ, 128), F32)], axis=0)
        matrices.append(left3(own, pad))

    row = lax.broadcasted_iota(jnp.int32, (splats, splats), 0)
    column = lax.broadcasted_iota(jnp.int32, (splats, splats), 1)
    ones = jnp.ones((splats, splats), BF16)
    lower = jnp.where(row < column, 1.0, 0.0).astype(BF16)
    upper = jnp.where(row > column, 1.0, 0.0).astype(BF16)
    for part in range(2):
        before[part * splats : (part + 1) * splats, :splats] = lower
        before[part * splats : (part + 1) * splats, splats:] = ones
        after_tri[part * splats : (part + 1) * splats, :splats] = upper
        after_tri[part * splats : (part + 1) * splats, splats:] = ones
    feats[...] = jnp.zeros(feats.shape, F32)

    for load in loads:
        load.wait()
    for camera in range(cameras):
        items = [(place, owner) for owner in range(owners) for place in range(cap)]
        for start in range(0, len(items), 2):
            couple = items[start : start + 2]
            right = jnp.concatenate(
                [right3(blocks[send_ref[camera, 0, place, owner]]) for place, owner in couple],
                axis=1,
            )
            result = dot32(matrices[camera], right)
            for number, (place, owner) in enumerate(couple):
                parcels[owner, camera * cap + place] = result[
                    :, number * splats : (number + 1) * splats
                ]

    pl.semaphore_wait(barrier, owners + groups - 2)
    raw_copies = []
    for step in range(1, owners):
        raw_copies.append(
            send(
                parcels.at[peer_dev[step], :, pl.ds(0, PROJ), :], raw.at[:, :, me, :],
                raw_sems.at[0, step - 1], raw_sems.at[1, step - 1], "dev", peer_dev[step],
            )
        )
    own_raw = keep(parcels.at[me, :, pl.ds(0, PROJ), :], raw.at[:, :, me, :], own_sems.at[0])
    meta_copies, moment_copies = [], []
    for turn in range(1, groups):
        meta_copies.append(
            send(
                meta.at[group], meta.at[group],
                meta_sems.at[0, turn - 1], meta_sems.at[1, turn - 1], "cam", peer_cam[turn],
            )
        )
    near = [lax.rem(group, 2) * -2 + 1 + group, lax.rem(group + 2, groups)]
    far = groups - 1 - group
    for kind, source in enumerate((first_hbm, second_hbm)):
        for side in range(2):
            moment_copies.append(
                send(
                    source, arrived.at[group, kind],
                    moment_sems.at[0, side, kind, 0], moment_sems.at[1, side, kind, 0],
                    "cam", near[side],
                )
            )
    own_moments = [
        keep(
            source.at[:, place, :],
            moments.at[kind, group * share + place, pl.ds(0, values), :],
            moment_sems.at[0, 0, kind, 1 + place],
        )
        for kind, source in enumerate((first_hbm, second_hbm))
        for place in range(share)
    ]

    one_hots = []
    entry_lane = lax.broadcasted_iota(jnp.int32, (slots, lists), 1)
    slot_row = lax.broadcasted_iota(jnp.int32, (slots, lists), 0)
    slot_row = lax.rem(slot_row, owners) * cap + lax.div(slot_row, owners)
    for camera in range(cameras):
        ids = jnp.full((slots, lists), -1, jnp.int32)
        for tile in range(tiles):
            for place in range(depth):
                slot = slot_ref[camera, tile, place]
                slot = jnp.where(place < count_ref[camera, tile], slot, -1)
                ids = jnp.where(entry_lane == tile * depth + place, slot, ids)
        hot = jnp.where(ids == slot_row, 1.0, 0.0)
        one_hots.append(jnp.concatenate([hot, hot], axis=1).astype(BF16))

    own_raw.wait()
    for copy in raw_copies:
        copy.wait_recv()
    for camera in range(cameras):
        for place in range(cap):
            make_features(raw, camera, place, cap, feats, saved)

    def render(camera, tile):
        render_tile(
            camera, tile, slot_ref, count_ref, target_ref, image_ref, feats, entries,
            weights, pairs, ratios, carry, before, after_tri, cot_rows, cot_cols, picture,
        )

    def slot_sums(camera):
        planes = []
        for start in range(0, PROJ, 2):
            kinds = list(range(start, min(start + 2, PROJ)))
            right = jnp.concatenate(
                [jnp.concatenate(split2(entries[k]), axis=0) for k in kinds], axis=1
            )
            result = dot32(one_hots[camera], right)
            for number in range(len(kinds)):
                planes.append(result[:, number * splats : (number + 1) * splats])
        for place in range(cap):
            part = [plane[place * owners : (place + 1) * owners] for plane in planes]
            return_planes(part, saved, camera * cap + place, back)

    back_copies = [[] for _ in range(cameras)]
    cross_copies = [[] for _ in range(cameras)]
    own_back = []

    def send_back(camera):
        mine = pl.ds(camera * cap, cap)
        for step in range(1, owners):
            back_copies[camera].append(
                send(
                    back.at[mine, :, peer_dev[step], :], gathered.at[group, mine, :, me, :],
                    back_sems.at[0, camera, step - 1], back_sems.at[1, camera, step - 1],
                    "dev", peer_dev[step],
                )
            )
        own_back.append(
            keep(
                back.at[mine, :, me, :], gathered.at[group, mine, :, me, :], own_sems.at[1 + camera]
            )
        )

    def send_across(camera):
        mine = pl.ds(camera * cap, cap)
        for step in range(owners):
            source = from_dev[step]
            if step:
                back_copies[camera][step - 1].wait_recv()
            else:
                own_back[camera].wait()
            piece = gathered.at[group, mine, :, source, :]
            for turn in range(1, groups):
                cross_copies[camera].append(
                    send(
                        piece, piece,
                        cross_sems.at[0, camera, turn - 1, step],
                        cross_sems.at[1, camera, turn - 1, step],
                        "cam", peer_cam[turn],
                    )
                )

    def scatter(turn, camera):
        origin = from_cam[turn]
        base = meta.shape[1] - 8
        ids = meta[origin, base + camera : base + camera + 1, :][:, :slots]
        block_row = lax.broadcasted_iota(jnp.int32, (owned, slots), 0).astype(F32)
        hot = jnp.where(jnp.broadcast_to(ids, (owned, slots)) == block_row, 1.0, 0.0)
        left = jnp.concatenate([hot, hot], axis=1).astype(BF16)
        for start in range(0, PROJ, 2):
            kinds = list(range(start, min(start + 2, PROJ)))
            sides = []
            for k in kinds:
                plane = jnp.concatenate(
                    [gathered[origin, camera * cap + place, k] for place in range(cap)], axis=0
                )
                sides.append(jnp.concatenate(split2(plane), axis=0))
            result = dot32(left, jnp.concatenate(sides, axis=1))
            for number, k in enumerate(kinds):
                flat_table[pl.ds((turn * cameras + camera) * PROJ + k, owned, stride=high_rows), :] = (
                    result[:, number * splats : (number + 1) * splats]
                )

    moment_moves = []

    def settle(kind, origin, side):
        for place in range(share):
            moment_moves.append(
                keep(
                    arrived.at[origin, kind, :, place, :],
                    moments.at[kind, origin * share + place, pl.ds(0, values), :],
                    moment_sems.at[1, side, kind, 1 + place],
                )
            )

    def pass_moments():
        for kind in range(2):
            for side in range(2):
                moment_copies[kind * 2 + side].wait_recv()
                origin = near[side]
                if side == kind:
                    moment_copies.append(
                        send(
                            arrived.at[origin, kind], arrived.at[origin, kind],
                            moment_sems.at[0, 2, kind, 0], moment_sems.at[1, 2, kind, 0],
                            "cam", near[1 - side],
                        )
                    )
                settle(kind, origin, side)

    for camera in range(cameras):
        for tile in range(tiles):
            render(camera, tile)
            if camera and tile == 0:
                send_across(camera - 1)
        if camera == 0:
            pass_moments()
        slot_sums(camera)
        send_back(camera)
    table[:, rows:high_rows, :] = jnp.zeros((owned, high_rows - rows, splats), F32)
    for copy in meta_copies:
        copy.wait_recv()
    stack = []
    for turn in range(groups):
        stack.append(meta[from_cam[turn], 0 : cameras * PROJ, :])
    stack.append(jnp.zeros((128 * -(-rows // 128) - rows, 128), F32))
    turned = jnp.concatenate(stack, axis=0).T
    left = left3(turned[:pad], high_rows)
    send_across(cameras - 1)
    for camera in range(cameras):
        scatter(0, camera)
    for camera in range(cameras):
        for turn in range(1, groups):
            for step in range(owners):
                cross_copies[camera][step * (groups - 1) + turn - 1].wait_recv()
            scatter(turn, camera)
    for kind in range(2):
        moment_copies[4 + kind].wait_recv()
        settle(kind, far, 2)
    for copy in own_moments + moment_moves:
        copy.wait()

    def gradients(couple):
        right = jnp.concatenate([right3(table[block]) for block in couple], axis=1)
        result = dot32(left, right)
        return [result[:, at * splats : (at + 1) * splats] for at in range(len(couple))]

    line = lax.broadcasted_iota(jnp.int32, (pad, splats), 0)
    for start in range(0, owners, 2):
        couple = list(range(start, min(start + 2, owners)))
        chosen = [split_ref[0, owner] for owner in couple]
        for owner, block, gradient in zip(couple, chosen, gradients(chosen)):
            alive = live_ref[0, owner].astype(F32)
            new_value, _, _ = adam(gradient, blocks[block], moments[0, block], moments[1, block])
            new_value = jnp.where(line < values, new_value, 1.0)
            parents[owner] = new_value * alive
    parent_copies = []
    for step in range(1, owners):
        parent_copies.append(
            send(
                parents.at[peer_dev[step], pl.ds(0, values + 1), :],
                landed.at[me, pl.ds(0, values + 1), :],
                parent_sems.at[0, step - 1], parent_sems.at[1, step - 1], "dev", peer_dev[step],
            )
        )
    own_parent = keep(
        parents.at[me, pl.ds(0, values + 1), :], landed.at[me, pl.ds(0, values + 1), :],
        own_sems.at[1 + cameras],
    )
    outs = []
    for start in range(0, owned, 2):
        couple = list(range(start, min(start + 2, owned)))
        for block, gradient in zip(couple, gradients(couple)):
            new_value, new_first, new_second = adam(
                gradient, blocks[block], moments[0, block], moments[1, block]
            )
            fresh[block] = new_value
            new_moments[0, block] = new_first
            new_moments[1, block] = new_second
            outs.append(
                keep(
                    fresh.at[block, pl.ds(0, values), :], params_out.at[:, block, :],
                    out_sems.at[block],
                )
            )
    for kind in range(2):
        for place in range(share):
            outs.append(
                keep(
                    new_moments.at[kind, group * share + place, pl.ds(0, values), :],
                    moments_out.at[kind, :, place, :],
                    moment_sems.at[0, 1, kind, 1 + place],
                )
            )
    for step in range(owners):
        source = from_dev[step]
        if step:
            parent_copies[step - 1].wait_recv()
        else:
            own_parent.wait()
        parent = landed[source]
        alive = parent[values : values + 1]
        shift = jnp.concatenate(
            [0.5 * jnp.exp(parent[0:8] - 1.0) * alive], axis=0
        )
        shift = jnp.concatenate([shift[3:6], jnp.zeros((pad - 3, splats), F32)], axis=0)
        shrunk = parent - jnp.where((line >= 3) & (line < 6), SHRINK, 0.0) * alive
        children[source, 0] = shrunk + shift
        children[source, 1] = shrunk - shift
        for kind in range(2):
            outs.append(
                keep(
                    children.at[source, kind, pl.ds(0, values), :],
                    child_out.at[source, :, kind, :],
                    child_sems.at[kind, step],
                )
            )
    for copy in outs:
        copy.wait()
    for copy in raw_copies + meta_copies + moment_copies + parent_copies:
        copy.wait_send()
    for camera in range(cameras):
        for copy in back_copies[camera] + cross_copies[camera]:
            copy.wait_send()


def spread_kernel(
    image_ref, fresh_ref, moments_ref, children_ref,
    image_out, params_out, first_out, second_out, child_out,
    fresh, moments, children, in_sems, out_sems,
):
    values = fresh.shape[0]
    owners = children.shape[0]
    trips = []
    for start in range(0, values, 15):
        some = pl.ds(start, min(15, values - start))
        trips.append((fresh_ref.at[some], fresh.at[some], params_out.at[some]))
    for start in range(0, owners, 4):
        some = pl.ds(start, min(4, owners - start))
        trips.append((children_ref.at[some], children.at[some], child_out.at[some]))
    for kind, target in enumerate((first_out, second_out)):
        trips.append((moments_ref.at[kind], moments.at[kind], target))
    started = [keep(src, mid, in_sems.at[at]) for at, (src, mid, _) in enumerate(trips)]
    image_out[...] = image_ref[...]
    outs = []
    for at, (_, mid, dst) in enumerate(trips):
        started[at].wait()
        outs.append(keep(mid, dst, out_sems.at[at]))
    for copy in outs:
        copy.wait()


def spread_out(images, fresh, new_moments, children):
    values, _, splats = fresh.shape
    owners = children.shape[0]
    shape = jax.ShapeDtypeStruct
    moments = shape(new_moments.shape[1:], F32)
    trips = -(-values // 15) + -(-owners // 4) + 2
    return pl.pallas_call(
        spread_kernel,
        out_shape=(
            shape(images.shape, F32),
            shape(fresh.shape, F32),
            moments,
            moments,
            shape(children.shape, F32),
        ),
        in_specs=[VMEM, ANY, ANY, ANY],
        out_specs=(VMEM, ANY, ANY, ANY, ANY),
        scratch_shapes=[
            pltpu.VMEM(fresh.shape, F32),
            pltpu.VMEM(new_moments.shape, F32),
            pltpu.VMEM(children.shape, F32),
            pltpu.SemaphoreType.DMA((trips,)),
            pltpu.SemaphoreType.DMA((trips,)),
        ],
        compiler_params=pltpu.CompilerParams(vmem_limit_bytes=BIG),
        name="spread",
    )(images, fresh, new_moments, children)


def body(
    params, moment_first, moment_second, cam_proj, send_block,
    tile_slot, tile_count, targets, split_block, split_live,
):
    groups = lax.axis_size("cam")
    cameras, _, values = cam_proj.shape
    owned, _, splats = params.shape
    share = moment_first.shape[2]
    owners, cap = send_block.shape[2:]
    _, tiles, depth = tile_slot.shape
    pixels = targets.shape[-1]
    depth = padded(depth, PAIR)
    pad = padded(values, 16)
    indices = cameras * cap
    rows = groups * cameras * PROJ
    high_rows = padded(rows, 16)
    meta_rows = padded(cameras * PROJ, 8) + 8
    by_value = lambda moment: moment[0, 0].transpose(1, 0, 2)
    shape = jax.ShapeDtypeStruct
    dma = pltpu.SemaphoreType.DMA
    scratch = [
        pltpu.VMEM((groups, meta_rows, 128), F32),
        pltpu.VMEM((owned, pad, splats), F32),
        pltpu.VMEM((2, owned, pad, splats), F32),
        pltpu.VMEM((groups, 2, values, share, splats), F32),
        pltpu.VMEM((owners, indices, 16, splats), F32),
        pltpu.VMEM((indices, PROJ, owners, splats), F32),
        pltpu.VMEM((indices * owners, 16, splats), F32),
        pltpu.VMEM((indices, SAVED, owners, splats), F32),
        pltpu.VMEM((PROJ, tiles * depth, splats), F32),
        pltpu.VMEM((indices, PROJ, owners, splats), F32),
        pltpu.VMEM((groups, indices, PROJ, owners, splats), F32),
        pltpu.VMEM((owned, high_rows, splats), F32),
        pltpu.VMEM((owned, pad, splats), F32),
        pltpu.VMEM((2, owned, pad, splats), F32),
        pltpu.VMEM((owners, pad, splats), F32),
        pltpu.VMEM((owners, pad, splats), F32),
        pltpu.VMEM((owners, 2, pad, splats), F32),
        pltpu.VMEM((depth, pixels, splats), F32),
        pltpu.VMEM((depth, pixels, 2 * splats), BF16),
        pltpu.VMEM((depth, pixels, splats), F32),
        pltpu.VMEM((pixels, splats), F32),
        pltpu.VMEM((2 * splats, 2 * splats), BF16),
        pltpu.VMEM((2 * splats, 2 * splats), BF16),
        pltpu.VMEM((16, pixels), BF16),
        pltpu.VMEM((pixels, 128), BF16),
        pltpu.VMEM((8, pixels), F32),
        dma((owned,)),
        dma((2, groups - 1)),
        dma((2, groups - 1, 2, 1 + share)),
        dma((2, owners - 1)),
        dma((2, cameras, owners - 1)),
        dma((2, cameras, groups - 1, owners)),
        dma((2, owners - 1)),
        dma((owned,)),
        dma((2, owners)),
        dma((2 + cameras,)),
    ]
    images, fresh, new_moments, children = pl.pallas_call(
        step_kernel,
        out_shape=(
            shape((cameras, 3, tiles, pixels), F32),
            shape((values, owned, splats), F32),
            shape((2, values, share, splats), F32),
            shape((owners, values, 2, splats), F32),
        ),
        in_specs=[SMEM] * 5 + [VMEM] * 2 + [ANY] * 3,
        out_specs=(VMEM, ANY, ANY, ANY),
        scratch_shapes=scratch,
        compiler_params=pltpu.CompilerParams(
            collective_id=5, has_side_effects=True, vmem_limit_bytes=BIG
        ),
        name="step",
    )(
        send_block.transpose(0, 1, 3, 2), tile_slot, tile_count, split_block, split_live,
        targets.transpose(0, 2, 1, 3), cam_proj.transpose(1, 0, 2),
        params.transpose(1, 0, 2), by_value(moment_first), by_value(moment_second),
    )
    images, new_params, new_first, new_second, children = spread_out(
        images, fresh, new_moments, children
    )
    restore = lambda moment: moment.transpose(1, 0, 2).reshape(moment_first.shape)
    return (
        images.transpose(0, 2, 1, 3),
        new_params.transpose(1, 0, 2),
        restore(new_first),
        restore(new_second),
        children.transpose(0, 2, 1, 3),
    )


def solution(mesh):
    placed = (
        P("dev", None, None),
        P("dev", "cam", None, None, None),
        P("dev", "cam", None, None, None),
        P("cam", None, None),
        P("cam", "dev", None, None),
        P("cam", "dev", None),
        P("cam", "dev"),
        P("cam", "dev", None, None),
        P("dev", None),
        P("dev", None),
    )
    return jax.shard_map(
        body,
        mesh=mesh,
        in_specs=placed,
        out_specs=(
            P("cam", "dev", None, None),
            P("dev", None, None),
            P("dev", "cam", None, None, None),
            P("dev", "cam", None, None, None),
            P("dev", None, None, None),
        ),
        check_vma=False,
    )
```
